32 devices in a mesh: uly: 2 (over x), blk: 16 (over z, y, core).
Axes of the slice: x: 2, y: 2, z: 4, core: 2. Of those that a mesh axis runs over, the one named last changes fastest.
Arguments:
- tokens: bfloat16 [4, 1024, 768], P('uly', 'blk'), may hold values from -6 to 6
- teacher: bfloat16 [4, 1024, 768], P('uly', 'blk'), may hold values from -6 to 6
- cotangent: bfloat16 [4, 1024, 768], P('uly', 'blk'), may hold values from -6 to 6
- valid: int32 [4, 1024], P('uly', 'blk'), may hold values from 0 to 1, as said below
- block_ids: int32 [4, 1024], replicated, may hold values from 0 to 7, never falling along the last dimension, each value on 1 to 256 neighbouring positions
- ln1_gain: float32 [768], replicated, may hold values from 0.1 to 1.9
- ln1_bias: float32 [768], replicated, may hold values from -1.5 to 1.5
- ln2_gain: float32 [768], replicated, may hold values from 0.1 to 1.9
- ln2_bias: float32 [768], replicated, may hold values from -1.5 to 1.5
- qkv_weight: bfloat16 [768, 896], P(('uly', 'blk')), may hold values from -0.3125 to 0.3125
- qkv_bias: float32 [896], replicated, may hold values from -1.5 to 1.5
- out_weight: bfloat16 [768, 768], P(('uly', 'blk')), may hold values from -1.25 to 1.25
- out_bias: float32 [768], replicated, may hold values from -1.5 to 1.5
- up_weight: bfloat16 [768, 3072], P(('uly', 'blk')), may hold values from -0.21875 to 0.21875
- up_bias: float32 [3072], replicated, may hold values from -2.5 to 2.5
- down_weight: bfloat16 [3072, 768], P(('uly', 'blk')), may hold values from -0.109375 to 0.109375
- down_bias: float32 [768], replicated, may hold values from -1.5 to 1.5
Outputs:
- activations: bfloat16 [4, 1024, 768], P('uly', 'blk')
- loss: float32 [], replicated
- tokens_grad: bfloat16 [4, 1024, 768], P('uly', 'blk')
- ln1_gain_grad: float32 [768], replicated
- ln1_bias_grad: float32 [768], replicated
- ln2_gain_grad: float32 [768], replicated
- ln2_bias_grad: float32 [768], replicated
- qkv_weight_grad: float32 [768, 896], P(('uly', 'blk'))
- qkv_bias_grad: float32 [896], replicated
- out_weight_grad: float32 [768, 768], P(('uly', 'blk'))
- out_bias_grad: float32 [768], replicated
- up_weight_grad: float32 [768, 3072], P(('uly', 'blk'))
- up_bias_grad: float32 [3072], replicated
- down_weight_grad: float32 [3072, 768], P(('uly', 'blk'))
- down_bias_grad: float32 [768], replicated
The draws below stay inside these ranges and needn't reach their ends.
Inputs may be any that keep to these rules, and one draw needn't show every extreme that they name: `block_ids`: within each sequence the block ids never fall, and each block is 1 to 256 consecutive tokens. The first token of every sequence is valid.
All inputs are finite; a program needn't handle non-finite values.
Results may differ from the reference program's by a relative error of at most 0.017.
Values may be sent and summed in bfloat16 or wider, within the bound.
A program may use at most 128 MiB of HBM per device.

```python
import math
import jax
import jax.numpy as jnp
import numpy as np
from jax import lax

D = 768
HEADS = 12
HD = 64
ROT = 16
FF = 3072
BLOCK = 256
LEN = 1024
SEQS = 4


def draw_valid(key, part):
    drawn = jax.random.randint(key, (SEQS, LEN), 0, 4 * LEN)
    place = lax.broadcasted_iota(jnp.int32, (SEQS, LEN), 1)
    live = jnp.logical_or(drawn < LEN + 2 * place, place == 0)
    return live.astype(jnp.int32)


def block_scale(own_key, shape, shards, least, high):
    factor_of, own = 1.0, jax.random.fold_in(own_key, 6)
    for dim, parts in shards:
        draws = jnp.exp(jax.random.uniform(jax.random.fold_in(own, dim), (parts,), jnp.float32, least / len(shards), high / len(shards)))
        factor_of = factor_of * jnp.repeat(draws, shape[dim] // parts).reshape([-1 if axis == dim else 1 for axis in range(len(shape))])
    return factor_of


def length_profile(amount, total, most, lean):
    portions = [(1 << 20) // math.isqrt(grade ** lean) + 1 for grade in range(2, amount + 1)]
    spare, given = total - most - (amount - 1), [1] * (amount - 1)
    while spare > 0:
        free = [i for i in range(amount - 1) if given[i] < most]
        mass, remaining = sum([portions[i] for i in free]), spare
        for i in free:
            extra = min(most - given[i], max(1, remaining * portions[i] // mass), spare)
            given[i] = given[i] + extra
            spare = spare - extra
    return np.array([most] + given)


def uneven_parts(stream_key, number_of, total, most, lean):
    if number_of == 2:
        one = jax.random.randint(stream_key, (), max(1, total - most), min(most, total - 1) + 1)
        return jnp.stack([one, total - one])
    sizes = jnp.asarray(length_profile(number_of, total, most, lean), jnp.int32)
    couples = (number_of - 1) // 2
    donor, taker = sizes[1:1 + 2 * couples:2], sizes[2:2 + 2 * couples:2]
    room = jnp.minimum(donor - 1, most - taker)
    shifted = jax.random.randint(jax.random.fold_in(stream_key, 1), (couples,), 0, 1 << 20) % (room + 1)
    sizes = sizes.at[1:1 + 2 * couples:2].set(donor - shifted).at[2:2 + 2 * couples:2].set(taker + shifted)
    return sizes[jax.random.permutation(jax.random.fold_in(stream_key, 2), number_of)]


def gaussian(own_key, extent, scale, reach, cuts=(), kind=jnp.bfloat16):
    level = block_scale(own_key, extent, cuts, -0.22, 0.18) if cuts else 1.0
    values = jax.random.normal(own_key, extent, jnp.float32) * scale * level
    return jnp.minimum(jnp.maximum(values, -reach), reach).astype(kind)


def setup_inputs(seed: int = 0) -> dict:
    streams_of = jax.random.split(jax.random.key(seed), 18)
    return {
        "tokens": gaussian(streams_of[0], (SEQS, LEN, D), 1.0, 6.0, ((0, 2), (1, 16))),
        "teacher": gaussian(streams_of[1], (SEQS, LEN, D), 1.0, 6.0, ((0, 2), (1, 16))),
        "cotangent": gaussian(streams_of[2], (SEQS, LEN, D), 1.0, 6.0, ((0, 2), (1, 16))),
        "valid": draw_valid(jax.random.fold_in(streams_of[17], 71), 0),
        "block_ids": jax.vmap(lambda own: jnp.searchsorted(jnp.cumsum(uneven_parts(own, 2 * LEN // BLOCK, LEN, BLOCK, 0)), jnp.arange(LEN), side="right"))(jax.random.split(streams_of[4], SEQS)).reshape((SEQS, LEN)).astype(jnp.int32),
        "ln1_gain": jnp.clip(1.0 + 0.18 * jax.random.normal(streams_of[5], (D,), jnp.float32), 0.1, 1.9),
        "ln1_bias": gaussian(streams_of[6], (D,), 0.3, 1.5, (), jnp.float32),
        "ln2_gain": jnp.clip(1.0 + 0.18 * jax.random.normal(streams_of[7], (D,), jnp.float32), 0.1, 1.9),
        "ln2_bias": gaussian(streams_of[8], (D,), 0.3, 1.5, (), jnp.float32),
        "qkv_weight": gaussian(streams_of[9], (D, D + 2 * HD), (D // 2) ** -0.5, 0.3125, ((0, 32),)),
        "qkv_bias": gaussian(streams_of[10], (D + 2 * HD,), 0.3, 1.5, (), jnp.float32),
        "out_weight": gaussian(streams_of[11], (D, D), (D // 32) ** -0.5, 1.25, ((0, 32),)),
        "out_bias": gaussian(streams_of[12], (D,), 0.3, 1.5, (), jnp.float32),
        "up_weight": gaussian(streams_of[13], (D, FF), D ** -0.5, 0.21875, ((0, 32),)),
        "up_bias": gaussian(streams_of[14], (FF,), 0.5, 2.5, (), jnp.float32),
        "down_weight": gaussian(streams_of[15], (FF, D), FF ** -0.5, 0.109375, ((0, 32),)),
        "down_bias": gaussian(streams_of[16], (D,), 0.3, 1.5, (), jnp.float32),
    }


norm_eps = 1e-05
highest = lax.Precision.HIGHEST

@jax.custom_vjp
def low(v):
    return lax.optimization_barrier(v.astype(jnp.bfloat16)).astype(jnp.float32)

@jax.custom_vjp
def low_back(v):
    return v

def low_keep(v):
    return (low(v), None)

def low_pass(kept, grad):
    return (grad,)

def back_keep(v):
    return (v, None)

def back_low(kept, grad):
    return (low(grad),)
low.defvjp(low_keep, low_pass)
low_back.defvjp(back_keep, back_low)

def layer_norm(values, gain, shift):
    center = values - lax.optimization_barrier(jnp.mean(values, -1, keepdims=True))
    spread = lax.optimization_barrier(jnp.mean(center * center, -1, keepdims=True))
    return center * lax.rsqrt(spread + norm_eps) * gain + shift

def gelu_exact(values):
    return 0.5 * values * (1.0 + lax.erf(values * 0.7071067811865476))

def rotary_tables(position):
    halfway = ROT // 2
    freqs = jnp.exp(-(jnp.arange(halfway, dtype=jnp.float32) * (2.0 / ROT)) * math.log(10000.0))
    angles = position.astype(jnp.float32)[:, None] * freqs[None, :]
    angles = jnp.concatenate([angles, angles], -1)
    return (jnp.cos(angles), jnp.sin(angles))

def rotate(values, cosine, sine):
    halfway = ROT // 2
    leading = values[..., :ROT]
    turned = jnp.concatenate([-leading[..., halfway:], leading[..., :halfway]], -1)
    return jnp.concatenate([leading * cosine + turned * sine, values[..., ROT:]], -1)

def attention(queries, keys, values, block_row):
    length = queries.shape[0]
    span_rows = math.gcd(length, 256)
    block_count = length // span_rows
    query_blocks = queries.reshape(block_count, span_rows, queries.shape[1], queries.shape[2])
    id_blocks = block_row.reshape(block_count, span_rows)

    @jax.checkpoint
    def one_block(paired):
        query_block, query_ids = paired
        scores = jnp.einsum('thd,kd->htk', query_block, keys, precision=highest) * 0.125
        scores = low_back(scores)
        allowed = block_row[None, None, :] <= query_ids[None, :, None]
        scores = jnp.where(allowed, scores, -1e+30)
        peak_score = lax.optimization_barrier(jnp.max(scores, -1, keepdims=True))
        exponent = jnp.exp(scores - peak_score)
        weights = exponent / lax.optimization_barrier(jnp.sum(exponent, -1, keepdims=True))
        weights = low(weights)
        return jnp.einsum('htk,kd->thd', weights, values, precision=highest)
    results = lax.map(one_block, (query_blocks, id_blocks))
    return results.reshape(length, queries.shape[1], queries.shape[2])

def sequence_forward(params, inputs, target, live, block_row):
    gain_one, shift_one, gain_two, shift_two, w_qkv, b_qkv, w_out, b_out, w_up, b_up, w_down, b_down = params
    length = inputs.shape[0]
    first_low = low(layer_norm(inputs, gain_one, shift_one))
    second_low = low(layer_norm(inputs, gain_two, shift_two))
    projected = jnp.dot(first_low, w_qkv, precision=highest) + b_qkv
    position = jnp.arange(length, dtype=jnp.int32)
    cosine, sine = rotary_tables(position)
    queries = low(rotate(low_back(projected[:, :D].reshape(length, HEADS, HD)), cosine[:, None, :], sine[:, None, :]))
    keys = low(rotate(low_back(projected[:, D:D + HD]), cosine, sine))
    values = low(low_back(projected[:, D + HD:]))
    attended = low(low_back(attention(queries, keys, values, block_row).reshape(length, D)))
    branch_attn = low_back(jnp.dot(attended, w_out, precision=highest) + b_out)
    hidden_pre = low_back(jnp.dot(second_low, w_up, precision=highest) + b_up)
    hidden_low = low(gelu_exact(hidden_pre))
    branch_ffn = low_back(jnp.dot(hidden_low, w_down, precision=highest) + b_down)
    result = inputs + branch_attn + branch_ffn
    difference = result - target
    error_sum = jnp.sum(lax.optimization_barrier(jnp.mean(difference * difference, -1)) * live)
    return (result, error_sum)

def reference(tokens, teacher, cotangent, valid, block_ids, ln1_gain, ln1_bias, ln2_gain, ln2_bias, qkv_weight, qkv_bias, out_weight, out_bias, up_weight, up_bias, down_weight, down_bias):
    params = tuple((member.astype(jnp.float32) for member in (ln1_gain, ln1_bias, ln2_gain, ln2_bias, qkv_weight, qkv_bias, out_weight, out_bias, up_weight, up_bias, down_weight, down_bias)))
    count = jnp.sum(valid.astype(jnp.float32))
    inverse = 1.0 / count

    def one_sequence(totals, item):
        rows, target, upstream, live, block_row = item

        def forward(weights, inputs):
            return sequence_forward(weights, inputs, target, live, block_row)
        (result, error_sum), pull = jax.vjp(forward, params, rows)
        weight_grads, row_grads = pull((upstream, inverse))
        totals = jax.tree.map(lambda earlier, update: earlier + update, totals, weight_grads)
        return (totals, (result.astype(jnp.bfloat16), error_sum, row_grads.astype(jnp.bfloat16)))
    zeros = jax.tree.map(jnp.zeros_like, params)
    items = (tokens.astype(jnp.float32), teacher.astype(jnp.float32), cotangent.astype(jnp.float32), valid.astype(jnp.float32), block_ids)
    totals, outputs = lax.scan(one_sequence, zeros, items)
    activations, error_sums, tokens_grad = outputs
    loss = jnp.sum(error_sums) / count
    return (activations, loss, tokens_grad, totals[0], totals[1], totals[2], totals[3], totals[4], totals[5], totals[6], totals[7], totals[8], totals[9], totals[10], totals[11])
```

```python
import math

import jax
import jax.numpy as jnp
from jax import lax
from jax.sharding import PartitionSpec as P

HD = 64
ROT = 16


norm_eps = 1e-05
BOTH = ("uly", "blk")


def layer_norm(values, gain, shift):
    center = values - jnp.mean(values, -1, keepdims=True)
    spread = jnp.mean(center * center, -1, keepdims=True)
    return center * lax.rsqrt(spread + norm_eps) * gain + shift


def gelu_exact(values):
    return 0.5 * values * (1.0 + lax.erf(values * 0.7071067811865476))


def rotary_tables(position):
    halfway = ROT // 2
    freqs = jnp.exp(-(jnp.arange(halfway, dtype=jnp.float32) * (2.0 / ROT)) * math.log(10000.0))
    angles = position.astype(jnp.float32)[:, None] * freqs[None, :]
    angles = jnp.concatenate([angles, angles], -1)
    return (jnp.cos(angles), jnp.sin(angles))


def rotate(values, cosine, sine):
    halfway = ROT // 2
    leading = values[..., :ROT]
    turned = jnp.concatenate([-leading[..., halfway:], leading[..., :halfway]], -1)
    return jnp.concatenate([leading * cosine + turned * sine, values[..., ROT:]], -1)


def rotate_back(grads, cosine, sine):
    halfway = ROT // 2
    leading = grads[..., :ROT]
    scaled = leading * sine
    turned = jnp.concatenate([scaled[..., halfway:], -scaled[..., :halfway]], -1)
    return jnp.concatenate([leading * cosine + turned, grads[..., ROT:]], -1)


def mm(pattern, a, b):
    return jnp.einsum(pattern, a, b, preferred_element_type=jnp.float32)


def scatter_sum(part):
    low = part.astype(jnp.bfloat16)
    return lax.psum_scatter(low, BOTH, scatter_dimension=0, tiled=True).astype(jnp.float32)


def general_layer(
    tokens,
    teacher,
    cotangent,
    valid,
    block_ids,
    ln1_gain,
    ln1_bias,
    ln2_gain,
    ln2_bias,
    qkv_weight,
    qkv_bias,
    out_weight,
    out_bias,
    up_weight,
    up_bias,
    down_weight,
    down_bias,
):
    seqs, shard_len, width = tokens.shape
    rows_here = seqs * shard_len
    heads = width // HD
    own_start = lax.axis_index("blk") * shard_len
    position = own_start + jnp.arange(shard_len, dtype=jnp.int32)
    cosine, sine = rotary_tables(position)
    inputs = tokens.astype(jnp.float32).reshape(rows_here, width)
    live_rows = valid.astype(jnp.float32).reshape(rows_here)
    live_count = lax.psum(jnp.sum(live_rows), BOTH)
    qkv_full, out_full, up_full, down_full = (
        lax.all_gather(w, BOTH, axis=0, tiled=True)
        for w in (qkv_weight, out_weight, up_weight, down_weight)
    )
    first_norm, first_pull = jax.vjp(layer_norm, inputs, ln1_gain, ln1_bias)
    second_norm, second_pull = jax.vjp(layer_norm, inputs, ln2_gain, ln2_bias)
    first_low = first_norm.astype(jnp.bfloat16)
    second_low = second_norm.astype(jnp.bfloat16)
    projected = jnp.dot(first_low, qkv_full, preferred_element_type=jnp.float32) + qkv_bias
    query_raw = projected[:, :width].reshape(seqs, shard_len, heads, HD)
    key_raw = projected[:, width : width + HD].reshape(seqs, shard_len, HD)
    value_raw = projected[:, width + HD :].reshape(seqs, shard_len, HD)
    query = rotate(query_raw, cosine[None, :, None, :], sine[None, :, None, :])
    query = query.astype(jnp.bfloat16)
    key_own = rotate(key_raw, cosine[None], sine[None]).astype(jnp.bfloat16)
    pair_own = jnp.concatenate([key_own, value_raw.astype(jnp.bfloat16)], -1)
    pair_all = lax.all_gather(pair_own, "blk", axis=1, tiled=True)
    length = pair_all.shape[1]
    stride = math.gcd(length, 1024)
    rows_att = heads * shard_len
    q_rows = query.transpose(0, 2, 1, 3).reshape(seqs, rows_att, HD)
    first_seq = lax.axis_index("uly") * seqs
    ids_all = lax.dynamic_slice_in_dim(block_ids, first_seq, seqs, 0)
    ids_own = lax.dynamic_slice_in_dim(ids_all, own_start, shard_len, 1)
    row_ids = jnp.tile(ids_own, (1, heads))
    last_ids = ids_own[:, shard_len - 1]

    def piece(counter):
        first = counter * stride
        pair = lax.dynamic_slice_in_dim(pair_all, first, stride, 1)
        ids = lax.dynamic_slice_in_dim(ids_all, first, stride, 1)
        return pair[..., :HD], pair[..., HD:], ids

    def scores_of(keys, ids):
        scores = mm("snd,srd->snr", keys, q_rows) * 0.125
        return scores, ids[:, :, None] <= row_ids[:, None, :]

    def forward_step(counter, state):
        keys, values, ids = piece(counter)

        def visit(state):
            maximum, weight_sum, accumulated = state
            scores, allowed = scores_of(keys, ids)
            scores = jnp.where(allowed, scores, -1e30)
            raised = jnp.maximum(maximum, jnp.max(scores, 1))
            factor = jnp.exp(maximum - raised)
            weights = jnp.where(allowed, jnp.exp(scores - raised[:, None, :]), 0.0)
            weight_sum = weight_sum * factor + jnp.sum(weights, 1)
            accumulated = accumulated * factor[:, None, :] + mm(
                "snr,snd->sdr", weights.astype(jnp.bfloat16), values
            )
            return (raised, weight_sum, accumulated)

        return lax.cond(jnp.any(ids[:, 0] <= last_ids), visit, lambda s: s, state)

    running_max, weight_sum, accumulated = lax.fori_loop(
        0,
        length // stride,
        forward_step,
        (
            jnp.full((seqs, rows_att), -1e30, jnp.float32),
            jnp.zeros((seqs, rows_att), jnp.float32),
            jnp.zeros((seqs, HD, rows_att), jnp.float32),
        ),
    )
    output_rows = accumulated / weight_sum[:, None, :]
    log_total = running_max + jnp.log(weight_sum)

    def to_tokens(rows):
        return (
            rows.reshape(seqs, HD, heads, shard_len).transpose(0, 3, 2, 1).reshape(rows_here, width)
        )

    attn_full = to_tokens(output_rows)
    attn_rows = attn_full.astype(jnp.bfloat16)
    branch_attn = jnp.dot(attn_rows, out_full, preferred_element_type=jnp.float32) + out_bias
    hidden_pre = jnp.dot(second_low, up_full, preferred_element_type=jnp.float32) + up_bias
    hidden_act, gelu_pull = jax.vjp(gelu_exact, hidden_pre)
    hidden_low = hidden_act.astype(jnp.bfloat16)
    branch_ffn = jnp.dot(hidden_low, down_full, preferred_element_type=jnp.float32) + down_bias
    result = inputs + branch_attn + branch_ffn
    difference = result - teacher.astype(jnp.float32).reshape(rows_here, width)
    error_local = jnp.sum(jnp.mean(difference * difference, -1) * live_rows)
    upstream = (
        cotangent.astype(jnp.float32).reshape(rows_here, width)
        + difference * (live_rows * (2.0 / width) / live_count)[:, None]
    )
    upstream_low = upstream.astype(jnp.bfloat16)
    down_grad = scatter_sum(mm("ri,rj->ij", hidden_low, upstream_low))
    output_bias_grad = jnp.sum(upstream_low.astype(jnp.float32), 0)
    hidden_grad = mm("rj,ij->ri", upstream_low, down_full)
    pre_grad = gelu_pull(hidden_grad)[0].astype(jnp.bfloat16)
    up_grad = scatter_sum(mm("ri,rj->ij", second_low, pre_grad))
    up_bias_grad = jnp.sum(pre_grad.astype(jnp.float32), 0)
    second_grad = mm("rj,ij->ri", pre_grad, up_full)
    out_grad = scatter_sum(mm("ri,rj->ij", attn_rows, upstream_low))
    attn_grad = mm("rj,ij->ri", upstream_low, out_full).astype(jnp.bfloat16)
    grad_tok = attn_grad.reshape(seqs, shard_len, heads, HD)
    grad_rows = grad_tok.transpose(0, 2, 1, 3).reshape(seqs, rows_att, HD)
    delta = jnp.sum(
        (attn_grad.astype(jnp.float32) * attn_full).reshape(seqs, shard_len, heads, HD), -1
    )
    delta = delta.transpose(0, 2, 1).reshape(seqs, rows_att)

    def backward_step(counter, state):
        keys, values, ids = piece(counter)

        def visit(state):
            query_acc, pair_acc = state
            scores, allowed = scores_of(keys, ids)
            probs = jnp.where(allowed, jnp.exp(scores - log_total[:, None, :]), 0.0)
            value_grad = mm("snr,srd->snd", probs.astype(jnp.bfloat16), grad_rows)
            prob_grad = mm("snd,srd->snr", values, grad_rows)
            score_grad = (probs * (prob_grad - delta[:, None, :])).astype(jnp.bfloat16)
            query_acc = query_acc + 0.125 * mm("snr,snd->sdr", score_grad, keys)
            key_grad = 0.125 * mm("snr,srd->snd", score_grad, q_rows)
            both = jnp.concatenate([key_grad, value_grad], -1).astype(jnp.bfloat16)
            return (query_acc, lax.dynamic_update_slice_in_dim(pair_acc, both, counter * stride, 1))

        return lax.cond(jnp.any(ids[:, 0] <= last_ids), visit, lambda s: s, state)

    query_acc, pair_grads = lax.fori_loop(
        0,
        length // stride,
        backward_step,
        (
            jnp.zeros((seqs, HD, rows_att), jnp.float32),
            jnp.zeros((seqs, length, 2 * HD), jnp.bfloat16),
        ),
    )
    pair_grads = lax.psum_scatter(pair_grads, "blk", scatter_dimension=1, tiled=True)
    pair_grads = pair_grads.astype(jnp.float32)
    query_grad = to_tokens(query_acc).reshape(seqs, shard_len, heads, HD)
    query_grad = rotate_back(query_grad, cosine[None, :, None, :], sine[None, :, None, :])
    key_grad = rotate_back(pair_grads[..., :HD], cosine[None], sine[None])
    qkv_grad_rows = jnp.concatenate(
        [
            query_grad.reshape(rows_here, width),
            key_grad.reshape(rows_here, HD),
            pair_grads[..., HD:].reshape(rows_here, HD),
        ],
        -1,
    ).astype(jnp.bfloat16)
    qkv_grad = scatter_sum(mm("ri,rj->ij", first_low, qkv_grad_rows))
    qkv_bias_grad = jnp.sum(qkv_grad_rows.astype(jnp.float32), 0)
    first_grad = mm("rj,ij->ri", qkv_grad_rows, qkv_full)
    input_one, gain_one, shift_one = first_pull(first_grad)
    input_two, gain_two, shift_two = second_pull(second_grad)
    tokens_grad = (
        (upstream + input_one + input_two).astype(jnp.bfloat16).reshape(seqs, shard_len, width)
    )
    vectors = (
        gain_one,
        shift_one,
        gain_two,
        shift_two,
        qkv_bias_grad,
        output_bias_grad,
        up_bias_grad,
        error_local,
    )
    vectors = lax.psum(vectors, BOTH)
    loss = vectors[7] / live_count
    activations = result.astype(jnp.bfloat16).reshape(seqs, shard_len, width)
    return (
        activations,
        loss,
        tokens_grad,
        vectors[0],
        vectors[1],
        vectors[2],
        vectors[3],
        qkv_grad,
        vectors[4],
        out_grad,
        vectors[5],
        up_grad,
        vectors[6],
        down_grad,
        vectors[5],
    )


def solution(mesh):
    tok = P("uly", "blk", None)
    row = P(("uly", "blk"), None)
    rep = P()
    return jax.shard_map(
        general_layer,
        mesh=mesh,
        in_specs=(tok, tok, tok, P("uly", "blk"), rep, rep, rep, rep, rep)
        + (row, rep, row, rep, row, rep, row, rep),
        out_specs=(tok, rep, tok, rep, rep, rep, rep, row, rep, row, rep, row, rep, row, rep),
        check_vma=False,
    )
```
